32 devices in a mesh: dp: 8 (over z, core), seq: 4 (over y, x).
Axes of the slice: x: 2, y: 2, z: 4, core: 2. Of those that a mesh axis runs over, the one named last changes fastest.
Arguments:
- waveform: bfloat16 [32, 2560], P('dp', 'seq'), may hold values from -6 to 6
- lengths: int32 [8, 4], P('dp'), may hold values from 1 to 2560, 6400 in all within a row
- conv_one: bfloat16 [10, 512], replicated, may hold values from -2 to 2
- conv_two: bfloat16 [1536, 512], replicated, may hold values from -0.15625 to 0.15625
- gain_one: float32 [512], replicated, may hold values from 0.1 to 1.9
- shift_one: float32 [512], replicated, may hold values from -3 to 3
- gain_two: float32 [512], replicated, may hold values from 0.1 to 1.9
- shift_two: float32 [512], replicated, may hold values from -3 to 3
- cotangent: bfloat16 [32, 256, 512], P('dp', 'seq'), may hold values from -0.0625 to 0.0625
Outputs:
- features: bfloat16 [32, 256, 512], P('dp', 'seq')
- conv_one_grad: float32 [10, 512], replicated
- conv_two_grad: float32 [1536, 512], P('seq')
- norm_grads: float32 [4, 512], replicated
The draws below stay inside these ranges and needn't reach their ends.
Inputs may be any that keep to these rules, and one draw needn't show every extreme that they name: In each row of lengths the 4 lengths sum to 6400 and the longest is exactly 2560.
All inputs are finite; a program needn't handle non-finite values.
Results may differ from the reference program's by a relative error of at most 0.0054.
Values may be sent and summed in bfloat16 or wider, within the bound.
A program may use at most 64 MiB of HBM per device.

```python
import math
import jax
import jax.numpy as jnp
import numpy as np
from jax import lax

CH = 512
CLIPS = 4
MAXLEN = 2560
F2 = 256
ALLCLIPS = 32
TOTLEN = 6400
N_DP = 8


def block_scale(rng, shape, split, low, high):
    level, own = 1.0, jax.random.fold_in(rng, 6)
    for dim, blocks in split:
        draws = jnp.exp(jax.random.uniform(jax.random.fold_in(own, dim), (blocks,), jnp.float32, low / len(split), high / len(split)))
        level = level * jnp.repeat(draws, shape[dim] // blocks).reshape([-1 if axis == dim else 1 for axis in range(len(shape))])
    return level


def length_profile(amount, total, limit, lean):
    loads = [(1 << 20) // math.isqrt(rank ** lean) + 1 for rank in range(2, amount + 1)]
    rest, given = total - limit - (amount - 1), [1] * (amount - 1)
    while rest > 0:
        movable = [i for i in range(amount - 1) if given[i] < limit]
        pool, budget = sum([loads[i] for i in movable]), rest
        for i in movable:
            more = min(limit - given[i], max(1, budget * loads[i] // pool), rest)
            given[i] = given[i] + more
            rest = rest - more
    return np.array([limit] + given)


def uneven_parts(rng, count, total, reach, lean):
    if count == 2:
        one = jax.random.randint(rng, (), max(1, total - reach), min(reach, total - 1) + 1)
        return jnp.stack([one, total - one])
    tallies = jnp.asarray(length_profile(count, total, reach, lean), jnp.int32)
    pairs = (count - 1) // 2
    source_of, receiver = tallies[1:1 + 2 * pairs:2], tallies[2:2 + 2 * pairs:2]
    room = jnp.minimum(source_of - 1, reach - receiver)
    moved = jax.random.randint(jax.random.fold_in(rng, 1), (pairs,), 0, 1 << 20) % (room + 1)
    tallies = tallies.at[1:1 + 2 * pairs:2].set(source_of - moved).at[2:2 + 2 * pairs:2].set(receiver + moved)
    return tallies[jax.random.permutation(jax.random.fold_in(rng, 2), count)]


def gaussian(own_key, dims, deviation, reach, shards=(), held_as=jnp.bfloat16):
    entries = jax.random.normal(own_key, dims, jnp.float32) * deviation
    if len(shards) > 0:
        entries = block_scale(own_key, dims, shards, -0.22, 0.18) * entries
    return jnp.clip(entries, min=-reach, max=reach).astype(held_as)


def setup_inputs(seed: int = 0) -> dict:
    streams_of = jax.random.split(jax.random.key(seed), 10)
    waveform = gaussian(streams_of[0], (ALLCLIPS, MAXLEN), 1.0, 6.0, ((0, 8), (1, 4)))
    lengths = jax.vmap(lambda own: uneven_parts(own, CLIPS, TOTLEN, MAXLEN, 2))(jax.random.split(streams_of[1], N_DP)).reshape((N_DP, CLIPS)).astype(jnp.int32)
    conv_one = gaussian(streams_of[2], (10, CH), 10 ** -0.5, 2.0)
    conv_two = gaussian(streams_of[3], (3 * CH, CH), (3 * CH) ** -0.5, 0.15625)
    gain_one = jnp.clip(1.0 + 0.18 * jax.random.normal(streams_of[4], (CH,), jnp.float32), 0.1, 1.9)
    shift_one = gaussian(streams_of[5], (CH,), 0.5, 3.0, (), jnp.float32)
    gain_two = jnp.clip(1.0 + 0.18 * jax.random.normal(streams_of[6], (CH,), jnp.float32), 0.1, 1.9)
    shift_two = gaussian(streams_of[7], (CH,), 0.5, 3.0, (), jnp.float32)
    cotangent = gaussian(streams_of[8], (ALLCLIPS, F2, CH), (ALLCLIPS * F2) ** -0.5, 0.0625, ((0, 8), (1, 4)))
    return dict(waveform=waveform, lengths=lengths, conv_one=conv_one, conv_two=conv_two, gain_one=gain_one, shift_one=shift_one, gain_two=gain_two, shift_two=shift_two, cotangent=cotangent)


epsilon = 1e-05
root_half = 0.7071067811865476
normal_peak = 0.3989422804014327

def norm_forward(preact, gain_vector, offset):
    centre = preact - lax.optimization_barrier(jnp.mean(preact, axis=-1, keepdims=True))
    inverse = lax.rsqrt(lax.optimization_barrier(jnp.mean(centre * centre, axis=-1, keepdims=True)) + epsilon)
    normed = centre * inverse
    return (normed, inverse, normed * gain_vector + offset)

def gelu_slope(values):
    return 0.5 * (1.0 + lax.erf(values * root_half)) + values * jnp.exp(-0.5 * values * values) * normal_peak

def norm_backward(upstream, normed, inverse, gain_vector):
    scaled = upstream * gain_vector
    return inverse * (scaled - lax.optimization_barrier(jnp.mean(scaled, axis=-1, keepdims=True)) - normed * lax.optimization_barrier(jnp.mean(scaled * normed, axis=-1, keepdims=True)))

def clip_pass(wave_clip, length, conv_one, conv_two, gain_one, shift_one, gain_two, shift_two, cot_clip):
    total_frames = wave_clip.shape[0] // 5
    half_frames = total_frames // 2
    channels = conv_two.shape[1]
    padded = jnp.concatenate([wave_clip, jnp.zeros((5,), wave_clip.dtype)])
    blocks = padded.reshape(total_frames + 1, 5)
    patch_one = jnp.concatenate([blocks[:-1], blocks[1:]], axis=1)
    pre_one = jnp.dot(patch_one, conv_one, preferred_element_type=jnp.float32)
    normed_one, inverse_one, output_one = norm_forward(pre_one, gain_one, shift_one)
    active_one = jax.nn.gelu(output_one, approximate=False).astype(jnp.bfloat16)
    widened = jnp.concatenate([active_one, jnp.zeros((1, channels), active_one.dtype)], axis=0)
    patch_two = jnp.concatenate([active_one.reshape(half_frames, 2 * channels), widened[2::2]], axis=1)
    pre_two = jnp.dot(patch_two, conv_two, preferred_element_type=jnp.float32)
    normed_two, inverse_two, output_two = norm_forward(pre_two, gain_two, shift_two)
    first_frames = (length - 5) // 5
    second_frames = (first_frames - 1) // 2
    validity = (jnp.arange(half_frames, dtype=jnp.int32) < second_frames).astype(output_two.dtype)[:, None]
    features = (jax.nn.gelu(output_two, approximate=False) * validity).astype(jnp.bfloat16)
    upstream_two = cot_clip.astype(output_two.dtype) * validity * gelu_slope(output_two)
    dpre_two = norm_backward(upstream_two, normed_two, inverse_two, gain_two).astype(jnp.bfloat16)
    grad_two = jnp.dot(patch_two.T, dpre_two, preferred_element_type=jnp.float32)
    dpatch_two = jnp.dot(dpre_two, conv_two.T, preferred_element_type=jnp.float32)
    paired = dpatch_two[:, :2 * channels].reshape(half_frames, 2, channels)
    onward = dpatch_two[:, 2 * channels:]
    carried = jnp.concatenate([jnp.zeros((1, channels), onward.dtype), onward[:-1]], axis=0)
    dact_one = jnp.stack([paired[:, 0] + carried, paired[:, 1]], axis=1).reshape(total_frames, channels)
    upstream_one = dact_one * gelu_slope(output_one)
    dpre_one = norm_backward(upstream_one, normed_one, inverse_one, gain_one)
    grad_one = jnp.dot(patch_one.astype(dpre_one.dtype).T, dpre_one, precision=lax.Precision.HIGHEST)
    norm_terms = jnp.stack([lax.optimization_barrier(jnp.sum(upstream_one * normed_one, 0)), lax.optimization_barrier(jnp.sum(upstream_one, 0)), lax.optimization_barrier(jnp.sum(upstream_two * normed_two, 0)), lax.optimization_barrier(jnp.sum(upstream_two, 0))])
    return (features, grad_one, grad_two, norm_terms)

def reference(waveform, lengths, conv_one, conv_two, gain_one, shift_one, gain_two, shift_two, cotangent):
    flat_lengths = lengths.reshape(-1)
    channels = conv_two.shape[1]

    def per_clip(totals, inputs):
        wave_clip, length, cot_clip = inputs
        features, grad_one, grad_two, norm_terms = clip_pass(wave_clip, length, conv_one, conv_two, gain_one, shift_one, gain_two, shift_two, cot_clip)
        return ((totals[0] + grad_one, totals[1] + grad_two, totals[2] + norm_terms), features)
    initial = (jnp.zeros((10, channels), jnp.float32), jnp.zeros((3 * channels, channels), jnp.float32), jnp.zeros((4, channels), jnp.float32))
    (sum_one, sum_two, sum_norms), features = lax.scan(per_clip, initial, (waveform, flat_lengths, cotangent))
    return (features, sum_one, sum_two, sum_norms)
```

```python
import functools

import jax
import jax.numpy as jnp
from jax import lax
from jax.experimental import pallas as pl
from jax.experimental.pallas import tpu as pltpu
from jax.sharding import PartitionSpec as P

MESH = pl.DeviceIdType.MESH
F32, BF16 = jnp.float32, jnp.bfloat16

epsilon = 1e-05
root_half = 0.7071067811865476
normal_peak = 0.3989422804014327

TAPS = 10
STEP = 32
PARTS = 2


def cdf(values):
    return 0.5 * (1.0 + lax.erf(values * root_half))


def slope_of(values, phi):
    return phi + values * jnp.exp(-0.5 * values * values) * normal_peak


def layer_norm(pre):
    centre = pre - jnp.mean(pre, axis=-1, keepdims=True)
    inverse = lax.rsqrt(jnp.mean(centre * centre, axis=-1, keepdims=True) + epsilon)
    return centre * inverse, inverse


def norm_backward(upstream, normed, inverse, gain):
    scaled = upstream * gain
    return inverse * (
        scaled
        - jnp.mean(scaled, axis=-1, keepdims=True)
        - normed * jnp.mean(scaled * normed, axis=-1, keepdims=True)
    )


def fold8(value):
    rows, channels = value.shape
    return jnp.sum(value.reshape(rows // 8, 8, channels), axis=0)


def dot_first(a, b):
    return lax.dot_general(a, b, (((0,), (0,)), ((), ())), preferred_element_type=F32)


def dot_last(a, b):
    return lax.dot_general(a, b, (((1,), (1,)), ((), ())), preferred_element_type=F32)


def kernel(
    ns, nz, pieces,
    wave, lengths, conv_one, conv_two, gain_one, shift_one, gain_two, shift_two, cot,
    features, grad_one_out, grad_two_out, norms_out,
    halo, patch, pre, hat, inv, phi, even, patch_two, pre_two, dpre_two, shifted, dact, dhi, dlo,
    mine, from_core, core_sum, from_seq, seq_sum, from_z, full,
    small, small_core, small_sum, small_seq, small_part, small_z,
    halo_s, halo_r, a_s, a_r, b_s, b_r, c_s, c_r, d_s, d_r, e_s, e_r,
    sa_s, sa_r, sb_s, sb_r, sc_s, sc_r,
):
    clips, samples = wave.shape
    channels = conv_two.shape[1]
    half = samples // (2 * 5)
    rows = clips * half
    share = mine.shape[3]
    width = mine.shape[4]
    piece = share // pieces

    pos = lax.axis_index("seq")
    dp = lax.axis_index("dp")
    z, core = dp // 2, lax.rem(dp, 2)
    partner = dp + 1 - 2 * core

    def at(dp_index, seq_index):
        return {"device_id": (dp_index, seq_index), "device_id_type": MESH}

    def seq_peer(d):
        return lax.rem(pos + d, ns)

    def z_peer(d):
        return lax.rem(z + d, nz)

    barrier = pltpu.get_barrier_semaphore()
    pl.semaphore_signal(barrier, inc=1, **at(partner, pos))
    for d in range(1, ns):
        pl.semaphore_signal(barrier, inc=1, **at(dp, seq_peer(d)))
    for d in range(1, nz):
        pl.semaphore_signal(barrier, inc=1, **at(2 * z_peer(d) + core, pos))

    g1, b1 = gain_one[...], shift_one[...]
    g2, b2 = gain_two[...], shift_two[...]
    taps = conv_one[...]

    def gather_frames(offset, source):
        total = source.shape[1]
        lane = lax.broadcasted_iota(jnp.int32, (half, total), 1) - offset - TAPS * lax.broadcasted_iota(
            jnp.int32, (half, total), 0
        )
        hit = (lane >= 0) & (lane < TAPS)
        picked = jnp.concatenate(
            [jnp.where(hit, source[c : c + 1, :], 0.0).astype(BF16) for c in range(clips)], axis=0
        )
        tap = lax.rem(
            lax.broadcasted_iota(jnp.int32, (total, 128), 0) + (TAPS - offset), TAPS
        )
        select = jnp.where(
            tap == lax.broadcasted_iota(jnp.int32, (total, 128), 1), 1.0, 0.0
        ).astype(BF16)
        return jnp.dot(picked, select, preferred_element_type=F32).astype(BF16)

    wave_f = wave[...].astype(F32)
    patch[0:rows] = gather_frames(0, wave_f)
    pre[0:rows] = jnp.dot(patch[0:rows, 0:TAPS], taps, preferred_element_type=F32)

    pl.semaphore_wait(barrier, ns + nz - 1)
    halo_copy = pltpu.make_async_remote_copy(
        wave.at[:, pl.ds(0, 128)], halo, halo_s, halo_r, **at(dp, lax.rem(pos + ns - 1, ns))
    )
    halo_copy.start()

    def forward_one(value):
        normed, inverse = layer_norm(value)
        out = normed * g1 + b1
        probability = cdf(out)
        return normed, inverse, probability, out * probability

    per_clip = half // STEP

    @pl.loop(0, rows // STEP)
    def _(i):
        r = pl.multiple_of(i * STEP, STEP)
        normed, inverse, probability, act = forward_one(pre[pl.ds(r, STEP)])
        hat[pl.ds(r, STEP)] = normed
        inv[pl.ds(r, STEP)] = jnp.broadcast_to(inverse, (STEP, 128))
        phi[pl.ds(r, STEP)] = probability
        even[i // per_clip, pl.ds(pl.multiple_of(lax.rem(i, per_clip) * STEP, STEP), STEP)] = act
        patch_two[pl.ds(r, STEP), pl.ds(0, channels)] = act.astype(BF16)

    halo_copy.wait()
    inside = jnp.where(pos < ns - 1, 1.0, 0.0).astype(F32)
    edge = (halo[...].astype(F32) * inside).astype(BF16)
    patch[rows : 2 * rows] = gather_frames(
        TAPS // 2, jnp.concatenate([wave_f, edge.astype(F32)], axis=1)
    )
    pre[rows : 2 * rows] = jnp.dot(patch[rows : 2 * rows, 0:TAPS], taps, preferred_element_type=F32)

    edge_pre = jnp.dot(edge[:, 0:TAPS], taps, preferred_element_type=F32)
    edge_hat, edge_inv, edge_phi, edge_act = forward_one(edge_pre)
    edge_act = edge_act * inside
    for c in range(clips):
        even[c, half : half + 1] = edge_act[c : c + 1]

    @pl.loop(rows // STEP, 2 * rows // STEP)
    def _(i):
        r = pl.multiple_of(i * STEP, STEP)
        normed, inverse, probability, act = forward_one(pre[pl.ds(r, STEP)])
        hat[pl.ds(r, STEP)] = normed
        inv[pl.ds(r, STEP)] = jnp.broadcast_to(inverse, (STEP, 128))
        phi[pl.ds(r, STEP)] = probability
        patch_two[pl.ds(pl.multiple_of(r - rows, STEP), STEP), pl.ds(channels, channels)] = act.astype(BF16)

    for c in range(clips):
        patch_two[c * half : (c + 1) * half, 2 * channels : 3 * channels] = even[
            c, 1 : half + 1
        ].astype(BF16)

    pre_two[...] = jnp.dot(patch_two[...], conv_two[...], preferred_element_type=F32)

    zeros8 = jnp.zeros((8, channels), F32)

    def second(i, sums):
        r = pl.multiple_of(i * STEP, STEP)
        normed, inverse = layer_norm(pre_two[pl.ds(r, STEP)])
        out = normed * g2 + b2
        probability = cdf(out)
        limit = lengths[0, i // per_clip] // 10 - 1
        frame = (
            pos * half
            + lax.rem(i, per_clip) * STEP
            + lax.broadcasted_iota(jnp.int32, (STEP, channels), 0)
        )
        valid = jnp.where(frame < limit, 1.0, 0.0).astype(F32)
        features[pl.ds(r, STEP)] = (out * probability * valid).astype(BF16)
        up = cot[pl.ds(r, STEP)].astype(F32) * valid * slope_of(out, probability)
        dpre_two[pl.ds(r, STEP)] = norm_backward(up, normed, inverse, g2).astype(BF16)
        return sums[0] + fold8(up * normed), sums[1] + fold8(up)

    two_hat, two_up = lax.fori_loop(0, rows // STEP, second, (zeros8, zeros8))

    down = dpre_two[...]
    for i in range(3 * channels // 384):
        product = dot_first(patch_two[:, i * 384 : (i + 1) * 384], down).astype(BF16)
        for j in range(384 // share):
            index = i * (384 // share) + j
            for q in range(PARTS):
                mine[q, index % 2, index // 2] = product[
                    j * share : (j + 1) * share, q * width : (q + 1) * width
                ]

    def core_copy(q):
        return pltpu.make_async_remote_copy(
            mine.at[q, 1 - core], from_core.at[q], a_s.at[q], a_r.at[q], **at(partner, pos)
        )

    def seq_copy(q, d):
        return pltpu.make_async_remote_copy(
            core_sum.at[q, d - 1], from_seq.at[q, d - 1], b_s.at[q, d - 1], b_r.at[q, d - 1],
            **at(dp, seq_peer(d)),
        )

    def z_rows(owner):
        return pl.ds(pl.multiple_of(owner * piece, piece), piece)

    def z_copy(q, d):
        return pltpu.make_async_remote_copy(
            seq_sum.at[q, z_rows(z_peer(d))], from_z.at[q, d - 1], c_s.at[q, d - 1], c_r.at[q, d - 1],
            **at(2 * z_peer(d) + core, pos),
        )

    def full_slice(q, which, owner):
        return full.at[q, which, z_rows(owner)]

    def spread_copy(q, d):
        there = full_slice(q, core, z)
        return pltpu.make_async_remote_copy(
            there, there, d_s.at[q, d - 1], d_r.at[q, d - 1], **at(2 * z_peer(d) + core, pos)
        )

    def relay_copy(q, d, which):
        there = full_slice(q, which, z_peer(d))
        return pltpu.make_async_remote_copy(
            there, there, e_s.at[q, d], e_r.at[q, d], **at(partner, pos)
        )

    def when_owner(owner, body):
        if pieces == nz:
            body()
        else:
            pl.when(owner < pieces)(body)

    for q in range(PARTS):
        core_copy(q).start()

    def to_seq(q):
        core_copy(q).wait()
        for d in range(1, ns):
            b = seq_peer(d)
            core_sum[q, d - 1] = (
                mine[q, core, b].astype(F32) + from_core[q, b].astype(F32)
            ).astype(BF16)
            seq_copy(q, d).start()

    def to_z(q):
        total = mine[q, core, pos].astype(F32) + from_core[q, pos].astype(F32)
        for d in range(1, ns):
            seq_copy(q, d).wait()
            total = total + from_seq[q, d - 1].astype(F32)
        seq_sum[q] = total.astype(BF16)
        for d in range(1, nz):
            when_owner(z_peer(d), lambda d=d: z_copy(q, d).start())

    def finish_z(q):
        def body():
            total = seq_sum[q, z_rows(z)].astype(F32)
            for d in range(1, nz):
                z_copy(q, d).wait_recv()
                total = total + from_z[q, d - 1].astype(F32)
            full[q, core, z_rows(z)] = total.astype(BF16)
            for d in range(1, nz):
                spread_copy(q, d).start()
            relay_copy(q, 0, core).start()

        when_owner(z, body)

    def relay(q):
        for d in range(1, nz):
            def body(d=d):
                spread_copy_from(q, d).wait_recv()
                relay_copy(q, nz - d, core).start()

            when_owner(z_peer(nz - d), body)

    def spread_copy_from(q, d):
        there = full_slice(q, core, z_peer(nz - d))
        return pltpu.make_async_remote_copy(
            there, there, d_s.at[q, d - 1], d_r.at[q, d - 1], **at(2 * z_peer(d) + core, pos)
        )

    for q in range(PARTS):
        to_seq(q)

    shifted[:, 0:8] = jnp.zeros((clips, 8, channels), F32)
    onward = dot_last(down, conv_two[2 * channels : 3 * channels])
    for c in range(clips):
        shifted[c, 8 : 8 + half] = onward[c * half : (c + 1) * half]
    first = dot_last(down, conv_two[0:channels])
    for c in range(clips):
        dact[c * half : (c + 1) * half] = first[c * half : (c + 1) * half] + shifted[c, 7 : 7 + half]
    dact[rows : 2 * rows] = dot_last(down, conv_two[channels : 2 * channels])

    def backward_one(incoming, normed, inverse, probability):
        up = incoming * slope_of(normed * g1 + b1, probability)
        return up, norm_backward(up, normed, inverse, g1)

    def back(i, sums):
        at_rows = pl.ds(pl.multiple_of(i * STEP, STEP), STEP)
        normed = hat[at_rows]
        up, dpre = backward_one(dact[at_rows], normed, inv[at_rows, 0:1], phi[at_rows])
        high = dpre.astype(BF16)
        dhi[at_rows] = high
        dlo[at_rows] = (dpre - high.astype(F32)).astype(BF16)
        return sums[0] + fold8(up * normed), sums[1] + fold8(up)

    one_hat, one_up = lax.fori_loop(0, 2 * rows // STEP, back, (zeros8, zeros8))

    edge_in = jnp.concatenate([shifted[c, 7 + half : 8 + half] for c in range(clips)], axis=0) * inside
    edge_up, edge_dpre = backward_one(edge_in, edge_hat, edge_inv, edge_phi)
    edge_high = edge_dpre.astype(BF16)
    edge_low = (edge_dpre - edge_high.astype(F32)).astype(BF16)

    frames = patch[...]
    grad_one = (
        dot_first(frames, dhi[...])
        + dot_first(frames, dlo[...])
    )[0:16] + (dot_first(edge, edge_high) + dot_first(edge, edge_low))[0:16]

    def total_row(value):
        return jnp.sum(value, axis=0, keepdims=True)

    small[...] = grad_one
    small[10:11] = total_row(one_hat) + total_row(edge_up * edge_hat)
    small[11:12] = total_row(one_up) + total_row(edge_up)
    small[12:13] = total_row(two_hat)
    small[13:14] = total_row(two_up)
    small[14:16] = jnp.zeros((2, channels), F32)

    small_core_copy = pltpu.make_async_remote_copy(small, small_core, sa_s, sa_r, **at(partner, pos))
    small_core_copy.start()

    def small_seq_copy(d):
        return pltpu.make_async_remote_copy(
            small_sum, small_seq.at[pos], sb_s.at[d - 1], sb_r.at[d - 1], **at(dp, seq_peer(d))
        )

    def small_z_copy(d):
        return pltpu.make_async_remote_copy(
            small_part, small_z.at[z], sc_s.at[d - 1], sc_r.at[d - 1], **at(2 * z_peer(d) + core, pos)
        )

    small_core_copy.wait()
    small_sum[...] = small[...] + small_core[...]
    for d in range(1, ns):
        small_seq_copy(d).start()
    small_seq[pos] = small_sum[...]

    to_z(0)

    for d in range(1, ns):
        small_seq_copy(d).wait()
    total = small_seq[0]
    for s in range(1, ns):
        total = total + small_seq[s]
    small_part[...] = total
    for d in range(1, nz):
        small_z_copy(d).start()
    small_z[z] = total

    for q in range(PARTS):
        if q > 0:
            to_z(q)
        finish_z(q)
    for q in range(PARTS):
        relay(q)

    for d in range(1, nz):
        small_z_copy(d).wait()
    total = small_z[0]
    for s in range(1, nz):
        total = total + small_z[s]
    grad_one_out[...] = total[0:TAPS]
    norms_out[...] = total[10:14]

    for q in range(PARTS):
        for d in range(1, nz):
            when_owner(z_peer(d), lambda d=d: z_copy(q, d).wait_send())

        def sent():
            for d in range(1, nz):
                spread_copy(q, d).wait_send()

        when_owner(z, sent)
        for d in range(nz):

            def relayed(d=d):
                relay_copy(q, d, core).wait_send()
                relay_copy(q, d, 1 - core).wait_recv()

            when_owner(z_peer(d), relayed)
        for h in range(2):
            grad_two_out[h * share : (h + 1) * share, q * width : (q + 1) * width] = full[q, h]


def on_device(ns, nz, waveform, lengths, conv_one, conv_two, gain_one, shift_one, gain_two, shift_two, cotangent):
    clips, samples = waveform.shape
    channels = conv_two.shape[1]
    half = cotangent.shape[1]
    rows = clips * half
    share = conv_two.shape[0] // ns // 2
    pieces = min(nz, share // 16)
    piece = share // pieces
    width = channels // PARTS
    dma = pltpu.SemaphoreType.DMA
    vmem = pl.BlockSpec(memory_space=pltpu.VMEM)
    features, grad_one, grad_two, norms = pl.pallas_call(
        functools.partial(kernel, ns, nz, pieces),
        out_shape=(
            jax.ShapeDtypeStruct((rows, channels), BF16),
            jax.ShapeDtypeStruct((TAPS, channels), F32),
            jax.ShapeDtypeStruct((2 * share, channels), BF16),
            jax.ShapeDtypeStruct((4, channels), F32),
        ),
        in_specs=[vmem, pl.BlockSpec(memory_space=pltpu.SMEM)] + [vmem] * 7,
        out_specs=(vmem,) * 4,
        scratch_shapes=[
            pltpu.VMEM((clips, 128), BF16),
            pltpu.VMEM((2 * rows, 128), BF16),
            pltpu.VMEM((2 * rows, channels), F32),
            pltpu.VMEM((2 * rows, channels), F32),
            pltpu.VMEM((2 * rows, 128), F32),
            pltpu.VMEM((2 * rows, channels), F32),
            pltpu.VMEM((clips, half + 8, channels), F32),
            pltpu.VMEM((rows, 3 * channels), BF16),
            pltpu.VMEM((rows, channels), F32),
            pltpu.VMEM((rows, channels), BF16),
            pltpu.VMEM((clips, half + 8, channels), F32),
            pltpu.VMEM((2 * rows, channels), F32),
            pltpu.VMEM((2 * rows, channels), BF16),
            pltpu.VMEM((2 * rows, channels), BF16),
            pltpu.VMEM((PARTS, 2, ns, share, width), BF16),
            pltpu.VMEM((PARTS, ns, share, width), BF16),
            pltpu.VMEM((PARTS, ns - 1, share, width), BF16),
            pltpu.VMEM((PARTS, ns - 1, share, width), BF16),
            pltpu.VMEM((PARTS, share, width), BF16),
            pltpu.VMEM((PARTS, nz - 1, piece, width), BF16),
            pltpu.VMEM((PARTS, 2, share, width), BF16),
            pltpu.VMEM((16, channels), F32),
            pltpu.VMEM((16, channels), F32),
            pltpu.VMEM((16, channels), F32),
            pltpu.VMEM((ns, 16, channels), F32),
            pltpu.VMEM((16, channels), F32),
            pltpu.VMEM((nz, 16, channels), F32),
            dma, dma,
            dma((PARTS,)), dma((PARTS,)),
            dma((PARTS, ns - 1)), dma((PARTS, ns - 1)),
            dma((PARTS, nz - 1)), dma((PARTS, nz - 1)),
            dma((PARTS, nz - 1)), dma((PARTS, nz - 1)),
            dma((PARTS, nz)), dma((PARTS, nz)),
            dma, dma,
            dma((ns - 1,)), dma((ns - 1,)),
            dma((nz - 1,)), dma((nz - 1,)),
        ],
        compiler_params=pltpu.CompilerParams(
            collective_id=0, has_side_effects=True, vmem_limit_bytes=48 * 1024 * 1024
        ),
    )(
        waveform,
        lengths,
        conv_one,
        conv_two,
        gain_one.reshape(1, channels),
        shift_one.reshape(1, channels),
        gain_two.reshape(1, channels),
        shift_two.reshape(1, channels),
        cotangent.reshape(rows, channels),
    )
    return features.reshape(clips, half, channels), grad_one, grad_two.astype(F32), norms


def solution(mesh):
    in_specs = (P("dp", "seq"), P("dp", None), P(), P(), P(), P(), P(), P(), P("dp", "seq", None))
    out_specs = (P("dp", "seq", None), P(), P("seq", None), P())
    return jax.shard_map(
        functools.partial(on_device, mesh.shape["seq"], mesh.shape["dp"] // 2),
        mesh=mesh, in_specs=in_specs, out_specs=out_specs, check_vma=False,
    )
```

```python
import functools

import jax
import jax.numpy as jnp
from jax import lax
from jax.experimental import pallas as pl
from jax.experimental.pallas import tpu as pltpu
from jax.sharding import PartitionSpec as P

MESH = pl.DeviceIdType.MESH
F32, BF16 = jnp.float32, jnp.bfloat16

epsilon = 1e-05
root_half = 0.7071067811865476
normal_peak = 0.3989422804014327

TAPS = 10
STEP = 32
PARTS = 2


def cdf(values):
    return 0.5 * (1.0 + lax.erf(values * root_half))


def slope_of(values, phi):
    return phi + values * jnp.exp(-0.5 * values * values) * normal_peak


def layer_norm(pre):
    centre = pre - jnp.mean(pre, axis=-1, keepdims=True)
    inverse = lax.rsqrt(jnp.mean(centre * centre, axis=-1, keepdims=True) + epsilon)
    return centre * inverse, inverse


def norm_backward(upstream, normed, inverse, gain):
    scaled = upstream * gain
    return inverse * (
        scaled
        - jnp.mean(scaled, axis=-1, keepdims=True)
        - normed * jnp.mean(scaled * normed, axis=-1, keepdims=True)
    )


def fold8(value):
    rows, channels = value.shape
    return jnp.sum(value.reshape(rows // 8, 8, channels), axis=0)


def dot_first(a, b):
    return lax.dot_general(a, b, (((0,), (0,)), ((), ())), preferred_element_type=F32)


def dot_last(a, b):
    return lax.dot_general(a, b, (((1,), (1,)), ((), ())), preferred_element_type=F32)


def kernel(
    ns, nz, pieces,
    wave_in, lengths_in, conv_one_in, conv_two_in, gain_one_in, shift_one_in, gain_two_in, shift_two_in, cot_in,
    features, grad_one_out, grad_two_out, norms_out,
    wave, lengths, conv_one, conv_two, gain_one, shift_one, gain_two, shift_two, cot, in_s,
    halo, patch, pre, hat, inv, phi, even, patch_two, pre_two, dpre_two, shifted, dact, dhi, dlo,
    mine, from_core, core_sum, from_seq, seq_sum, from_z, full,
    small, small_core, small_sum, small_seq, small_part, small_z,
    halo_s, halo_r, a_s, a_r, b_s, b_r, c_s, c_r, d_s, d_r, e_s, e_r,
    sa_s, sa_r, sb_s, sb_r, sc_s, sc_r,
):
    clips, samples = wave.shape
    channels = conv_two.shape[1]
    half = samples // (2 * 5)
    rows = clips * half
    share = mine.shape[3]
    width = mine.shape[4]
    piece = share // pieces

    pos = lax.axis_index("seq")
    dp = lax.axis_index("dp")
    z, core = dp // 2, lax.rem(dp, 2)
    partner = dp + 1 - 2 * core

    def at(dp_index, seq_index):
        return {"device_id": (dp_index, seq_index), "device_id_type": MESH}

    def seq_peer(d):
        return lax.rem(pos + d, ns)

    def z_peer(d):
        return lax.rem(z + d, nz)

    loads = [
        pltpu.make_async_copy(source, target, in_s.at[i])
        for i, (source, target) in enumerate(
            (
                (wave_in, wave),
                (conv_one_in, conv_one),
                (gain_one_in, gain_one),
                (shift_one_in, shift_one),
                (conv_two_in, conv_two),
                (gain_two_in, gain_two),
                (shift_two_in, shift_two),
                (lengths_in, lengths),
                (cot_in, cot),
            )
        )
    ]
    for load in loads:
        load.start()
    barrier = pltpu.get_barrier_semaphore()
    pl.semaphore_signal(barrier, inc=1, **at(partner, pos))
    for d in range(1, ns):
        pl.semaphore_signal(barrier, inc=1, **at(dp, seq_peer(d)))
    for d in range(1, nz):
        pl.semaphore_signal(barrier, inc=1, **at(2 * z_peer(d) + core, pos))

    for load in loads[:4]:
        load.wait()
    g1, b1 = gain_one[...], shift_one[...]
    taps = conv_one[...]

    def gather_frames(offset, source):
        total = source.shape[1]
        lane = lax.broadcasted_iota(jnp.int32, (half, total), 1) - offset - TAPS * lax.broadcasted_iota(
            jnp.int32, (half, total), 0
        )
        hit = (lane >= 0) & (lane < TAPS)
        picked = jnp.concatenate(
            [jnp.where(hit, source[c : c + 1, :], 0.0).astype(BF16) for c in range(clips)], axis=0
        )
        tap = lax.rem(
            lax.broadcasted_iota(jnp.int32, (total, 128), 0) + (TAPS - offset), TAPS
        )
        select = jnp.where(
            tap == lax.broadcasted_iota(jnp.int32, (total, 128), 1), 1.0, 0.0
        ).astype(BF16)
        return jnp.dot(picked, select, preferred_element_type=F32)

    wave_f = wave[...].astype(F32)
    for parity in range(2):
        found = gather_frames(parity * TAPS // 2, wave_f)
        patch[parity * rows : (parity + 1) * rows] = found
        pre[parity * rows : (parity + 1) * rows] = jnp.dot(
            found.astype(BF16)[:, 0:TAPS], taps, preferred_element_type=F32
        )

    pl.semaphore_wait(barrier, ns + nz - 1)
    halo_copy = pltpu.make_async_remote_copy(
        wave.at[:, pl.ds(0, 128)], halo, halo_s, halo_r, **at(dp, lax.rem(pos + ns - 1, ns))
    )
    halo_copy.start()

    def forward_one(value):
        normed, inverse = layer_norm(value)
        out = normed * g1 + b1
        probability = cdf(out)
        return normed, inverse, probability, out * probability

    per_clip = half // STEP

    @pl.loop(0, rows // STEP)
    def _(i):
        r = pl.multiple_of(i * STEP, STEP)
        normed, inverse, probability, act = forward_one(pre[pl.ds(r, STEP)])
        hat[pl.ds(r, STEP)] = normed
        inv[pl.ds(r, STEP)] = jnp.broadcast_to(inverse, (STEP, 128))
        phi[pl.ds(r, STEP)] = probability
        even[i // per_clip, pl.ds(pl.multiple_of(lax.rem(i, per_clip) * STEP, STEP), STEP)] = act
        patch_two[pl.ds(r, STEP), pl.ds(0, channels)] = act.astype(BF16)

    def odd_rows(block):
        r = pl.multiple_of(rows + block * STEP, STEP)
        normed, inverse, probability, act = forward_one(pre[pl.ds(r, STEP)])
        hat[pl.ds(r, STEP)] = normed
        inv[pl.ds(r, STEP)] = jnp.broadcast_to(inverse, (STEP, 128))
        phi[pl.ds(r, STEP)] = probability
        patch_two[pl.ds(pl.multiple_of(block * STEP, STEP), STEP), pl.ds(channels, channels)] = act.astype(BF16)

    @pl.loop(0, clips * (per_clip - 1))
    def _(i):
        odd_rows(i // (per_clip - 1) * per_clip + lax.rem(i, per_clip - 1))

    halo_copy.wait()
    inside = jnp.where(pos < ns - 1, 1.0, 0.0).astype(F32)
    edge = (halo[...].astype(F32) * inside).astype(BF16)
    moved = lax.broadcasted_iota(jnp.int32, (128, 128), 0) + TAPS // 2
    tap = lax.broadcasted_iota(jnp.int32, (128, 128), 1)
    fix = jnp.dot(
        edge,
        jnp.where((moved == tap) & (tap < TAPS), 1.0, 0.0).astype(BF16),
        preferred_element_type=F32,
    )
    fix_pre = jnp.dot(fix.astype(BF16)[:, 0:TAPS], taps, preferred_element_type=F32)
    for c in range(clips):
        last = rows + (c + 1) * half - 1
        patch[last : last + 1] = patch[last : last + 1] + fix[c : c + 1]
        pre[last : last + 1] = pre[last : last + 1] + fix_pre[c : c + 1]

    edge_pre = jnp.dot(edge[:, 0:TAPS], taps, preferred_element_type=F32)
    edge_hat, edge_inv, edge_phi, edge_act = forward_one(edge_pre)
    edge_act = edge_act * inside
    for c in range(clips):
        even[c, half : half + 1] = edge_act[c : c + 1]

    @pl.loop(0, clips)
    def _(c):
        odd_rows(c * per_clip + per_clip - 1)

    for c in range(clips):
        patch_two[c * half : (c + 1) * half, 2 * channels : 3 * channels] = even[
            c, 1 : half + 1
        ].astype(BF16)

    for load in loads[4:]:
        load.wait()
    g2, b2 = gain_two[...], shift_two[...]
    pre_two[...] = jnp.dot(patch_two[...], conv_two[...], preferred_element_type=F32)

    zeros8 = jnp.zeros((8, channels), F32)

    def second(i, sums):
        r = pl.multiple_of(i * STEP, STEP)
        normed, inverse = layer_norm(pre_two[pl.ds(r, STEP)])
        out = normed * g2 + b2
        probability = cdf(out)
        limit = lengths[0, i // per_clip] // 10 - 1
        frame = (
            pos * half
            + lax.rem(i, per_clip) * STEP
            + lax.broadcasted_iota(jnp.int32, (STEP, channels), 0)
        )
        valid = jnp.where(frame < limit, 1.0, 0.0).astype(F32)
        features[pl.ds(r, STEP)] = (out * probability * valid).astype(BF16)
        up = cot[pl.ds(r, STEP)].astype(F32) * valid * slope_of(out, probability)
        dpre_two[pl.ds(r, STEP)] = norm_backward(up, normed, inverse, g2).astype(BF16)
        return sums[0] + fold8(up * normed), sums[1] + fold8(up)

    two_hat, two_up = lax.fori_loop(0, rows // STEP, second, (zeros8, zeros8))

    down = dpre_two[...]
    for i in range(3 * channels // 384):
        product = dot_first(patch_two[:, i * 384 : (i + 1) * 384], down).astype(BF16)
        for j in range(384 // share):
            index = i * (384 // share) + j
            for q in range(PARTS):
                mine[q, index % 2, index // 2] = product[
                    j * share : (j + 1) * share, q * width : (q + 1) * width
                ]

    def core_copy(q):
        return pltpu.make_async_remote_copy(
            mine.at[q, 1 - core], from_core.at[q], a_s.at[q], a_r.at[q], **at(partner, pos)
        )

    def seq_copy(q, d):
        return pltpu.make_async_remote_copy(
            core_sum.at[q, d - 1], from_seq.at[q, d - 1], b_s.at[q, d - 1], b_r.at[q, d - 1],
            **at(dp, seq_peer(d)),
        )

    def z_rows(owner):
        return pl.ds(pl.multiple_of(owner * piece, piece), piece)

    def z_copy(q, d):
        return pltpu.make_async_remote_copy(
            seq_sum.at[q, z_rows(z_peer(d))], from_z.at[q, d - 1], c_s.at[q, d - 1], c_r.at[q, d - 1],
            **at(2 * z_peer(d) + core, pos),
        )

    def full_slice(q, which, owner):
        return full.at[q, which, z_rows(owner)]

    def spread_copy(q, d):
        there = full_slice(q, core, z)
        return pltpu.make_async_remote_copy(
            there, there, d_s.at[q, d - 1], d_r.at[q, d - 1], **at(2 * z_peer(d) + core, pos)
        )

    def relay_copy(q, d, which):
        there = full_slice(q, which, z_peer(d))
        return pltpu.make_async_remote_copy(
            there, there, e_s.at[q, d], e_r.at[q, d], **at(partner, pos)
        )

    def when_owner(owner, body):
        if pieces == nz:
            body()
        else:
            pl.when(owner < pieces)(body)

    for q in range(PARTS):
        core_copy(q).start()

    def to_seq(q):
        core_copy(q).wait()
        for d in range(1, ns):
            b = seq_peer(d)
            core_sum[q, d - 1] = (
                mine[q, core, b].astype(F32) + from_core[q, b].astype(F32)
            ).astype(BF16)
            seq_copy(q, d).start()

    def to_z(q):
        total = mine[q, core, pos].astype(F32) + from_core[q, pos].astype(F32)
        for d in range(1, ns):
            seq_copy(q, d).wait()
            total = total + from_seq[q, d - 1].astype(F32)
        seq_sum[q] = total.astype(BF16)
        for d in range(1, nz):
            when_owner(z_peer(d), lambda d=d: z_copy(q, d).start())

    def finish_z(q):
        def body():
            total = seq_sum[q, z_rows(z)].astype(F32)
            for d in range(1, nz):
                z_copy(q, d).wait_recv()
                total = total + from_z[q, d - 1].astype(F32)
            full[q, core, z_rows(z)] = total.astype(BF16)
            for d in range(1, nz):
                spread_copy(q, d).start()
            relay_copy(q, 0, core).start()

        when_owner(z, body)

    def relay(q):
        for d in range(1, nz):
            def body(d=d):
                spread_copy_from(q, d).wait_recv()
                relay_copy(q, nz - d, core).start()

            when_owner(z_peer(nz - d), body)

    def spread_copy_from(q, d):
        there = full_slice(q, core, z_peer(nz - d))
        return pltpu.make_async_remote_copy(
            there, there, d_s.at[q, d - 1], d_r.at[q, d - 1], **at(2 * z_peer(d) + core, pos)
        )

    for q in range(PARTS):
        to_seq(q)

    shifted[:, 0:8] = jnp.zeros((clips, 8, channels), F32)
    onward = dot_last(down, conv_two[2 * channels : 3 * channels])
    for c in range(clips):
        shifted[c, 8 : 8 + half] = onward[c * half : (c + 1) * half]
    first = dot_last(down, conv_two[0:channels])
    for c in range(clips):
        dact[c * half : (c + 1) * half] = first[c * half : (c + 1) * half] + shifted[c, 7 : 7 + half]
    dact[rows : 2 * rows] = dot_last(down, conv_two[channels : 2 * channels])

    def backward_one(incoming, normed, inverse, probability):
        up = incoming * slope_of(normed * g1 + b1, probability)
        return up, norm_backward(up, normed, inverse, g1)

    def back(i, sums):
        at_rows = pl.ds(pl.multiple_of(i * STEP, STEP), STEP)
        normed = hat[at_rows]
        up, dpre = backward_one(dact[at_rows], normed, inv[at_rows, 0:1], phi[at_rows])
        high = dpre.astype(BF16)
        dhi[at_rows] = high
        dlo[at_rows] = (dpre - high.astype(F32)).astype(BF16)
        return sums[0] + fold8(up * normed), sums[1] + fold8(up)

    one_hat, one_up = lax.fori_loop(0, 2 * rows // STEP, back, (zeros8, zeros8))

    edge_in = jnp.concatenate([shifted[c, 7 + half : 8 + half] for c in range(clips)], axis=0) * inside
    edge_up, edge_dpre = backward_one(edge_in, edge_hat, edge_inv, edge_phi)
    edge_high = edge_dpre.astype(BF16)
    edge_low = (edge_dpre - edge_high.astype(F32)).astype(BF16)

    frames = patch[...].astype(BF16)
    grad_one = (
        dot_first(frames, dhi[...])
        + dot_first(frames, dlo[...])
    )[0:16] + (dot_first(edge, edge_high) + dot_first(edge, edge_low))[0:16]

    def total_row(value):
        return jnp.sum(value, axis=0, keepdims=True)

    small[...] = grad_one
    small[10:11] = total_row(one_hat) + total_row(edge_up * edge_hat)
    small[11:12] = total_row(one_up) + total_row(edge_up)
    small[12:13] = total_row(two_hat)
    small[13:14] = total_row(two_up)
    small[14:16] = jnp.zeros((2, channels), F32)

    small_core_copy = pltpu.make_async_remote_copy(small, small_core, sa_s, sa_r, **at(partner, pos))
    small_core_copy.start()

    def small_seq_copy(d):
        return pltpu.make_async_remote_copy(
            small_sum, small_seq.at[pos], sb_s.at[d - 1], sb_r.at[d - 1], **at(dp, seq_peer(d))
        )

    def small_z_copy(d):
        return pltpu.make_async_remote_copy(
            small_part, small_z.at[z], sc_s.at[d - 1], sc_r.at[d - 1], **at(2 * z_peer(d) + core, pos)
        )

    small_core_copy.wait()
    small_sum[...] = small[...] + small_core[...]
    for d in range(1, ns):
        small_seq_copy(d).start()
    small_seq[pos] = small_sum[...]

    to_z(0)

    for d in range(1, ns):
        small_seq_copy(d).wait()
    total = small_seq[0]
    for s in range(1, ns):
        total = total + small_seq[s]
    small_part[...] = total
    for d in range(1, nz):
        small_z_copy(d).start()
    small_z[z] = total

    for q in range(1, PARTS + 2):
        if q < PARTS:
            to_z(q)
        if q - 1 < PARTS:
            finish_z(q - 1)
        if q > 1:
            relay(q - 2)

    for d in range(1, nz):
        small_z_copy(d).wait()
    total = small_z[0]
    for s in range(1, nz):
        total = total + small_z[s]
    grad_one_out[...] = total[0:TAPS]
    norms_out[...] = total[10:14]

    for q in range(PARTS):
        for d in range(1, nz):
            when_owner(z_peer(d), lambda d=d: z_copy(q, d).wait_send())

        def sent():
            for d in range(1, nz):
                spread_copy(q, d).wait_send()

        when_owner(z, sent)
        for d in range(nz):

            def relayed(d=d):
                relay_copy(q, d, core).wait_send()
                relay_copy(q, d, 1 - core).wait_recv()

            when_owner(z_peer(d), relayed)
        for h in range(2):
            grad_two_out[h * share : (h + 1) * share, q * width : (q + 1) * width] = full[q, h]


def on_device(ns, nz, waveform, lengths, conv_one, conv_two, gain_one, shift_one, gain_two, shift_two, cotangent):
    clips, samples = waveform.shape
    channels = conv_two.shape[1]
    half = cotangent.shape[1]
    rows = clips * half
    share = conv_two.shape[0] // ns // 2
    pieces = min(nz, share // 16)
    piece = share // pieces
    width = channels // PARTS
    dma = pltpu.SemaphoreType.DMA
    vmem = pl.BlockSpec(memory_space=pltpu.VMEM)
    hbm = pl.BlockSpec(memory_space=pltpu.HBM)
    features, grad_one, grad_two, norms = pl.pallas_call(
        functools.partial(kernel, ns, nz, pieces),
        out_shape=(
            jax.ShapeDtypeStruct((rows, channels), BF16),
            jax.ShapeDtypeStruct((TAPS, channels), F32),
            jax.ShapeDtypeStruct((2 * share, channels), BF16),
            jax.ShapeDtypeStruct((4, channels), F32),
        ),
        in_specs=[hbm] * 9,
        out_specs=(vmem,) * 4,
        scratch_shapes=[
            pltpu.VMEM(waveform.shape, BF16),
            pltpu.SMEM(lengths.shape, jnp.int32),
            pltpu.VMEM(conv_one.shape, BF16),
            pltpu.VMEM(conv_two.shape, BF16),
            pltpu.VMEM((1, channels), F32),
            pltpu.VMEM((1, channels), F32),
            pltpu.VMEM((1, channels), F32),
            pltpu.VMEM((1, channels), F32),
            pltpu.VMEM((rows, channels), BF16),
            dma((9,)),
            pltpu.VMEM((clips, 128), BF16),
            pltpu.VMEM((2 * rows, 128), F32),
            pltpu.VMEM((2 * rows, channels), F32),
            pltpu.VMEM((2 * rows, channels), F32),
            pltpu.VMEM((2 * rows, 128), F32),
            pltpu.VMEM((2 * rows, channels), F32),
            pltpu.VMEM((clips, half + 8, channels), F32),
            pltpu.VMEM((rows, 3 * channels), BF16),
            pltpu.VMEM((rows, channels), F32),
            pltpu.VMEM((rows, channels), BF16),
            pltpu.VMEM((clips, half + 8, channels), F32),
            pltpu.VMEM((2 * rows, channels), F32),
            pltpu.VMEM((2 * rows, channels), BF16),
            pltpu.VMEM((2 * rows, channels), BF16),
            pltpu.VMEM((PARTS, 2, ns, share, width), BF16),
            pltpu.VMEM((PARTS, ns, share, width), BF16),
            pltpu.VMEM((PARTS, ns - 1, share, width), BF16),
            pltpu.VMEM((PARTS, ns - 1, share, width), BF16),
            pltpu.VMEM((PARTS, share, width), BF16),
            pltpu.VMEM((PARTS, nz - 1, piece, width), BF16),
            pltpu.VMEM((PARTS, 2, share, width), BF16),
            pltpu.VMEM((16, channels), F32),
            pltpu.VMEM((16, channels), F32),
            pltpu.VMEM((16, channels), F32),
            pltpu.VMEM((ns, 16, channels), F32),
            pltpu.VMEM((16, channels), F32),
            pltpu.VMEM((nz, 16, channels), F32),
            dma, dma,
            dma((PARTS,)), dma((PARTS,)),
            dma((PARTS, ns - 1)), dma((PARTS, ns - 1)),
            dma((PARTS, nz - 1)), dma((PARTS, nz - 1)),
            dma((PARTS, nz - 1)), dma((PARTS, nz - 1)),
            dma((PARTS, nz)), dma((PARTS, nz)),
            dma, dma,
            dma((ns - 1,)), dma((ns - 1,)),
            dma((nz - 1,)), dma((nz - 1,)),
        ],
        compiler_params=pltpu.CompilerParams(
            collective_id=0, has_side_effects=True, vmem_limit_bytes=48 * 1024 * 1024
        ),
    )(
        *[
            pltpu.with_memory_space_constraint(value, pltpu.HBM)
            for value in (
        waveform,
        lengths,
        conv_one,
        conv_two,
        gain_one.reshape(1, channels),
        shift_one.reshape(1, channels),
        gain_two.reshape(1, channels),
        shift_two.reshape(1, channels),
        cotangent.reshape(rows, channels),
    )])
    features, grad_one, grad_two, norms = pl.pallas_call(
        put_out,
        out_shape=(
            jax.ShapeDtypeStruct((rows, channels), BF16),
            jax.ShapeDtypeStruct((TAPS, channels), F32),
            jax.ShapeDtypeStruct((2 * share, channels), F32),
            jax.ShapeDtypeStruct((4, channels), F32),
        ),
        in_specs=[vmem] * 4,
        out_specs=(hbm,) * 4,
        scratch_shapes=[pltpu.VMEM((2 * share, channels), F32), dma((4,))],
        compiler_params=pltpu.CompilerParams(vmem_limit_bytes=4 * 1024 * 1024),
    )(features, grad_one, grad_two, norms)
    return features.reshape(clips, half, channels), grad_one, grad_two, norms


def put_out(features, grad_one, grad_two, norms, features_out, grad_one_out, grad_two_out, norms_out, wide, sem):
    copies = [
        pltpu.make_async_copy(source, target, sem.at[i])
        for i, (source, target) in enumerate(
            (
                (features, features_out),
                (grad_one, grad_one_out),
                (norms, norms_out),
                (wide, grad_two_out),
            )
        )
    ]
    for copy in copies[:3]:
        copy.start()
    wide[...] = grad_two[...].astype(F32)
    copies[3].start()
    for copy in copies:
        copy.wait()


def solution(mesh):
    in_specs = (P("dp", "seq"), P("dp", None), P(), P(), P(), P(), P(), P(), P("dp", "seq", None))
    out_specs = (P("dp", "seq", None), P(), P("seq", None), P())
    return jax.shard_map(
        functools.partial(on_device, mesh.shape["seq"], mesh.shape["dp"] // 2),
        mesh=mesh, in_specs=in_specs, out_specs=out_specs, check_vma=False,
    )
```

```python
import functools

import jax
import jax.numpy as jnp
from jax import lax
from jax.experimental import pallas as pl
from jax.experimental.pallas import tpu as pltpu
from jax.sharding import PartitionSpec as P

MESH = pl.DeviceIdType.MESH
F32, BF16 = jnp.float32, jnp.bfloat16

epsilon = 1e-05
root_half = 0.7071067811865476
normal_peak = 0.3989422804014327

TAPS = 10
STEP = 32
PARTS = 2


def cdf(values):
    return 0.5 * (1.0 + lax.erf(values * root_half))


def slope_of(values, phi):
    return phi + values * jnp.exp(-0.5 * values * values) * normal_peak


def layer_norm(pre):
    centre = pre - jnp.mean(pre, axis=-1, keepdims=True)
    inverse = lax.rsqrt(jnp.mean(centre * centre, axis=-1, keepdims=True) + epsilon)
    return centre * inverse, inverse


def norm_backward(upstream, normed, inverse, gain):
    scaled = upstream * gain
    return inverse * (
        scaled
        - jnp.mean(scaled, axis=-1, keepdims=True)
        - normed * jnp.mean(scaled * normed, axis=-1, keepdims=True)
    )


def fold8(value):
    rows, channels = value.shape
    return jnp.sum(value.reshape(rows // 8, 8, channels), axis=0)


def dot_first(a, b):
    return lax.dot_general(a, b, (((0,), (0,)), ((), ())), preferred_element_type=F32)


def dot_last(a, b):
    return lax.dot_general(a, b, (((1,), (1,)), ((), ())), preferred_element_type=F32)


def kernel(
    ns, nz, pieces,
    wave_in, lengths_in, conv_one_in, conv_two_in, gain_one_in, shift_one_in, gain_two_in, shift_two_in, cot_in,
    features, grad_one_out, grad_two_out, norms_out,
    wave, lengths, conv_one, conv_two, gain_one, shift_one, gain_two, shift_two, cot, in_s,
    halo, patch, pre, hat, inv, phi, even, patch_two, pre_two, dpre_two, shifted, dact, dhi, dlo,
    mine, from_core, core_sum, from_seq, seq_sum, from_z, full,
    small, small_core, small_sum, small_seq, small_part, small_z, small_all,
    halo_s, halo_r, a_s, a_r, b_s, b_r, c_s, c_r, d_s, d_r, e_s, e_r,
    sa_s, sa_r, sb_s, sb_r, sc_s, sc_r, sd_s, sd_r,
):
    clips, samples = wave.shape
    channels = conv_two.shape[1]
    half = samples // (2 * 5)
    rows = clips * half
    share = mine.shape[3]
    width = mine.shape[4]
    piece = share // pieces

    pos = lax.axis_index("seq")
    dp = lax.axis_index("dp")
    z, core = dp // 2, lax.rem(dp, 2)
    partner = dp + 1 - 2 * core

    def at(dp_index, seq_index):
        return {"device_id": (dp_index, seq_index), "device_id_type": MESH}

    def seq_peer(d):
        return lax.rem(pos + d, ns)

    def z_peer(d):
        return lax.rem(z + d, nz)

    loads = [
        pltpu.make_async_copy(source, target, in_s.at[i])
        for i, (source, target) in enumerate(
            (
                (wave_in, wave),
                (conv_one_in, conv_one),
                (gain_one_in, gain_one),
                (shift_one_in, shift_one),
                (conv_two_in, conv_two),
                (gain_two_in, gain_two),
                (shift_two_in, shift_two),
                (lengths_in, lengths),
                (cot_in, cot),
            )
        )
    ]
    for load in loads:
        load.start()
    barrier = pltpu.get_barrier_semaphore()
    pl.semaphore_signal(barrier, inc=1, **at(partner, pos))
    for d in range(1, ns):
        pl.semaphore_signal(barrier, inc=1, **at(dp, seq_peer(d)))
    for d in range(1, nz):
        pl.semaphore_signal(barrier, inc=1, **at(2 * z_peer(d) + core, pos))

    for load in loads[:4]:
        load.wait()
    g1, b1 = gain_one[...], shift_one[...]
    taps = conv_one[...]

    def gather_frames(offset, source):
        total = source.shape[1]
        lane = lax.broadcasted_iota(jnp.int32, (half, total), 1) - offset - TAPS * lax.broadcasted_iota(
            jnp.int32, (half, total), 0
        )
        hit = (lane >= 0) & (lane < TAPS)
        picked = jnp.concatenate(
            [jnp.where(hit, source[c : c + 1, :], 0.0).astype(BF16) for c in range(clips)], axis=0
        )
        tap = lax.rem(
            lax.broadcasted_iota(jnp.int32, (total, 128), 0) + (TAPS - offset), TAPS
        )
        select = jnp.where(
            tap == lax.broadcasted_iota(jnp.int32, (total, 128), 1), 1.0, 0.0
        ).astype(BF16)
        return jnp.dot(picked, select, preferred_element_type=F32)

    wave_f = wave[...].astype(F32)
    for parity in range(2):
        found = gather_frames(parity * TAPS // 2, wave_f)
        patch[parity * rows : (parity + 1) * rows] = found
        pre[parity * rows : (parity + 1) * rows] = jnp.dot(
            found.astype(BF16)[:, 0:TAPS], taps, preferred_element_type=F32
        )

    def forward_one(value):
        normed, inverse = layer_norm(value)
        out = normed * g1 + b1
        probability = cdf(out)
        return normed, inverse, probability, out * probability

    per_clip = half // STEP

    def even_rows(i):
        r = pl.multiple_of(i * STEP, STEP)
        normed, inverse, probability, act = forward_one(pre[pl.ds(r, STEP)])
        hat[pl.ds(r, STEP)] = normed
        inv[pl.ds(r, STEP)] = jnp.broadcast_to(inverse, (STEP, 128))
        phi[pl.ds(r, STEP)] = probability
        even[i // per_clip, pl.ds(pl.multiple_of(lax.rem(i, per_clip) * STEP, STEP), STEP)] = act
        patch_two[pl.ds(r, STEP), pl.ds(0, channels)] = act.astype(BF16)

    blocks = rows // STEP
    pl.loop(0, blocks // 2)(even_rows)

    pl.semaphore_wait(barrier, ns + nz - 1)
    halo_copy = pltpu.make_async_remote_copy(
        wave.at[:, pl.ds(0, 128)], halo, halo_s, halo_r, **at(dp, lax.rem(pos + ns - 1, ns))
    )
    halo_copy.start()

    pl.loop(blocks // 2, blocks)(even_rows)

    def odd_rows(block):
        r = pl.multiple_of(rows + block * STEP, STEP)
        normed, inverse, probability, act = forward_one(pre[pl.ds(r, STEP)])
        hat[pl.ds(r, STEP)] = normed
        inv[pl.ds(r, STEP)] = jnp.broadcast_to(inverse, (STEP, 128))
        phi[pl.ds(r, STEP)] = probability
        patch_two[pl.ds(pl.multiple_of(block * STEP, STEP), STEP), pl.ds(channels, channels)] = act.astype(BF16)

    @pl.loop(0, clips * (per_clip - 1))
    def _(i):
        odd_rows(i // (per_clip - 1) * per_clip + lax.rem(i, per_clip - 1))

    halo_copy.wait()
    inside = jnp.where(pos < ns - 1, 1.0, 0.0).astype(F32)
    edge = (halo[...].astype(F32) * inside).astype(BF16)
    moved = lax.broadcasted_iota(jnp.int32, (128, 128), 0) + TAPS // 2
    tap = lax.broadcasted_iota(jnp.int32, (128, 128), 1)
    fix = jnp.dot(
        edge,
        jnp.where((moved == tap) & (tap < TAPS), 1.0, 0.0).astype(BF16),
        preferred_element_type=F32,
    )
    fix_pre = jnp.dot(fix.astype(BF16)[:, 0:TAPS], taps, preferred_element_type=F32)
    for c in range(clips):
        last = rows + (c + 1) * half - 1
        patch[last : last + 1] = patch[last : last + 1] + fix[c : c + 1]
        pre[last : last + 1] = pre[last : last + 1] + fix_pre[c : c + 1]

    edge_pre = jnp.dot(edge[:, 0:TAPS], taps, preferred_element_type=F32)
    edge_hat, edge_inv, edge_phi, edge_act = forward_one(edge_pre)
    edge_act = edge_act * inside
    for c in range(clips):
        even[c, half : half + 1] = edge_act[c : c + 1]

    @pl.loop(0, clips)
    def _(c):
        odd_rows(c * per_clip + per_clip - 1)

    for c in range(clips):
        patch_two[c * half : (c + 1) * half, 2 * channels : 3 * channels] = even[
            c, 1 : half + 1
        ].astype(BF16)

    for load in loads[4:]:
        load.wait()
    g2, b2 = gain_two[...], shift_two[...]
    pre_two[...] = jnp.dot(patch_two[...], conv_two[...], preferred_element_type=F32)

    zeros8 = jnp.zeros((8, channels), F32)

    def second(i, sums):
        r = pl.multiple_of(i * STEP, STEP)
        normed, inverse = layer_norm(pre_two[pl.ds(r, STEP)])
        out = normed * g2 + b2
        probability = cdf(out)
        limit = lengths[0, i // per_clip] // 10 - 1
        frame = (
            pos * half
            + lax.rem(i, per_clip) * STEP
            + lax.broadcasted_iota(jnp.int32, (STEP, channels), 0)
        )
        valid = jnp.where(frame < limit, 1.0, 0.0).astype(F32)
        features[pl.ds(r, STEP)] = (out * probability * valid).astype(BF16)
        up = cot[pl.ds(r, STEP)].astype(F32) * valid * slope_of(out, probability)
        dpre_two[pl.ds(r, STEP)] = norm_backward(up, normed, inverse, g2).astype(BF16)
        return sums[0] + fold8(up * normed), sums[1] + fold8(up)

    two_hat, two_up = lax.fori_loop(0, rows // STEP, second, (zeros8, zeros8))

    down = dpre_two[...]
    def core_copy(q, d):
        b = seq_peer(d)
        return pltpu.make_async_remote_copy(
            mine.at[q, 1 - core, b], from_core.at[q, b], a_s.at[q, d], a_r.at[q, d], **at(partner, pos)
        )

    def seq_copy(q, d):
        return pltpu.make_async_remote_copy(
            core_sum.at[q, d - 1], from_seq.at[q, d - 1], b_s.at[q, d - 1], b_r.at[q, d - 1],
            **at(dp, seq_peer(d)),
        )

    def z_rows(owner):
        return pl.ds(pl.multiple_of(owner * piece, piece), piece)

    def z_copy(q, d):
        return pltpu.make_async_remote_copy(
            seq_sum.at[q, z_rows(z_peer(d))], from_z.at[q, d - 1], c_s.at[q, d - 1], c_r.at[q, d - 1],
            **at(2 * z_peer(d) + core, pos),
        )

    def full_slice(q, which, owner):
        return full.at[q, which, z_rows(owner)]

    def spread_copy(q, d):
        there = full_slice(q, core, z)
        return pltpu.make_async_remote_copy(
            there, there, d_s.at[q, d - 1], d_r.at[q, d - 1], **at(2 * z_peer(d) + core, pos)
        )

    def relay_copy(q, d, which):
        there = full_slice(q, which, z_peer(d))
        return pltpu.make_async_remote_copy(
            there, there, e_s.at[q, d], e_r.at[q, d], **at(partner, pos)
        )

    def when_owner(owner, body):
        if pieces == nz:
            body()
        else:
            pl.when(owner < pieces)(body)

    for q in range(PARTS):
        for i in range(3 * channels // 384):
            product = dot_first(
                patch_two[:, i * 384 : (i + 1) * 384], down[:, q * width : (q + 1) * width]
            ).astype(BF16)
            for j in range(384 // share):
                index = i * (384 // share) + j
                mine[q, index % 2, index // 2] = product[j * share : (j + 1) * share]
        for d in [*range(1, ns), 0]:
            core_copy(q, d).start()

    def to_seq(q):
        for d in range(1, ns):
            b = seq_peer(d)
            core_copy(q, d).wait()
            core_sum[q, d - 1] = (
                mine[q, core, b].astype(F32) + from_core[q, b].astype(F32)
            ).astype(BF16)
            seq_copy(q, d).start()

    def to_z(q):
        core_copy(q, 0).wait()
        total = mine[q, core, pos].astype(F32) + from_core[q, pos].astype(F32)
        for d in range(1, ns):
            seq_copy(q, d).wait()
            total = total + from_seq[q, d - 1].astype(F32)
        seq_sum[q] = total.astype(BF16)
        for d in range(1, nz):
            when_owner(z_peer(d), lambda d=d: z_copy(q, d).start())

    def finish_z(q):
        def body():
            total = seq_sum[q, z_rows(z)].astype(F32)
            for d in range(1, nz):
                z_copy(q, d).wait_recv()
                total = total + from_z[q, d - 1].astype(F32)
            full[q, core, z_rows(z)] = total.astype(BF16)
            for d in range(1, nz):
                spread_copy(q, d).start()
            relay_copy(q, 0, core).start()

        when_owner(z, body)

    def relay(q):
        for d in range(1, nz):
            def body(d=d):
                spread_copy_from(q, d).wait_recv()
                relay_copy(q, nz - d, core).start()

            when_owner(z_peer(nz - d), body)

    def spread_copy_from(q, d):
        there = full_slice(q, core, z_peer(nz - d))
        return pltpu.make_async_remote_copy(
            there, there, d_s.at[q, d - 1], d_r.at[q, d - 1], **at(2 * z_peer(d) + core, pos)
        )

    for q in range(PARTS):
        to_seq(q)

    shifted[:, 0:8] = jnp.zeros((clips, 8, channels), F32)
    onward = dot_last(down, conv_two[2 * channels : 3 * channels])
    for c in range(clips):
        shifted[c, 8 : 8 + half] = onward[c * half : (c + 1) * half]
    first = dot_last(down, conv_two[0:channels])
    for c in range(clips):
        dact[c * half : (c + 1) * half] = first[c * half : (c + 1) * half] + shifted[c, 7 : 7 + half]
    dact[rows : 2 * rows] = dot_last(down, conv_two[channels : 2 * channels])

    def backward_one(incoming, normed, inverse, probability):
        up = incoming * slope_of(normed * g1 + b1, probability)
        return up, norm_backward(up, normed, inverse, g1)

    def back(i, sums):
        at_rows = pl.ds(pl.multiple_of(i * STEP, STEP), STEP)
        normed = hat[at_rows]
        up, dpre = backward_one(dact[at_rows], normed, inv[at_rows, 0:1], phi[at_rows])
        high = dpre.astype(BF16)
        dhi[at_rows] = high
        dlo[at_rows] = (dpre - high.astype(F32)).astype(BF16)
        return sums[0] + fold8(up * normed), sums[1] + fold8(up)

    one_hat, one_up = lax.fori_loop(0, 2 * rows // STEP, back, (zeros8, zeros8))

    edge_in = jnp.concatenate([shifted[c, 7 + half : 8 + half] for c in range(clips)], axis=0) * inside
    edge_up, edge_dpre = backward_one(edge_in, edge_hat, edge_inv, edge_phi)
    edge_high = edge_dpre.astype(BF16)
    edge_low = (edge_dpre - edge_high.astype(F32)).astype(BF16)

    frames = patch[...].astype(BF16)
    grad_one = (
        dot_first(frames, dhi[...])
        + dot_first(frames, dlo[...])
    )[0:16] + (dot_first(edge, edge_high) + dot_first(edge, edge_low))[0:16]

    def total_row(value):
        return jnp.sum(value, axis=0, keepdims=True)

    middle = channels // 2
    sums = (
        (0, grad_one),
        (10, total_row(one_hat) + total_row(edge_up * edge_hat)),
        (11, total_row(one_up) + total_row(edge_up)),
        (12, total_row(two_hat)),
        (13, total_row(two_up)),
        (14, jnp.zeros((2, channels), F32)),
    )
    for row, value in sums:
        for h in range(2):
            small[h, row : row + value.shape[0]] = value[:, h * middle : (h + 1) * middle]

    small_core_copy = pltpu.make_async_remote_copy(
        small.at[1 - core], small_core, sa_s, sa_r, **at(partner, pos)
    )
    small_core_copy.start()

    def small_seq_copy(d):
        return pltpu.make_async_remote_copy(
            small_sum, small_seq.at[pos], sb_s.at[d - 1], sb_r.at[d - 1], **at(dp, seq_peer(d))
        )

    def small_z_copy(d):
        return pltpu.make_async_remote_copy(
            small_part, small_z.at[z], sc_s.at[d - 1], sc_r.at[d - 1], **at(2 * z_peer(d) + core, pos)
        )

    def small_done_copy(which):
        return pltpu.make_async_remote_copy(
            small_all.at[which], small_all.at[which], sd_s, sd_r, **at(partner, pos)
        )

    to_z(0)

    small_core_copy.wait()
    value = (small[core] + small_core[...]).astype(BF16)
    small_sum[...] = value
    small_seq[pos] = value
    for d in range(1, ns):
        small_seq_copy(d).start()

    for q in range(1, PARTS + 2):
        if q < PARTS:
            to_z(q)
        if q == max(PARTS - 1, 1):
            for d in range(1, ns):
                small_seq_copy(d).wait()
            total = small_seq[0].astype(F32)
            for p in range(1, ns):
                total = total + small_seq[p].astype(F32)
            value = total.astype(BF16)
            small_part[...] = value
            small_z[z] = value
            for d in range(1, nz):
                small_z_copy(d).start()
        if q - 1 < PARTS:
            finish_z(q - 1)
        if q == PARTS:
            for d in range(1, nz):
                small_z_copy(d).wait()
            total = small_z[0].astype(F32)
            for p in range(1, nz):
                total = total + small_z[p].astype(F32)
            small_all[core] = total
            small_done_copy(core).start()
        if q > 1:
            relay(q - 2)

    small_done_copy(core).wait_send()
    small_done_copy(1 - core).wait_recv()
    for h in range(2):
        grad_one_out[:, h * middle : (h + 1) * middle] = small_all[h, 0:TAPS]
        norms_out[:, h * middle : (h + 1) * middle] = small_all[h, 10:14]

    for q in range(PARTS):
        for d in range(1, nz):
            when_owner(z_peer(d), lambda d=d: z_copy(q, d).wait_send())

        def sent():
            for d in range(1, nz):
                spread_copy(q, d).wait_send()

        when_owner(z, sent)
        for d in range(nz):

            def relayed(d=d):
                relay_copy(q, d, core).wait_send()
                relay_copy(q, d, 1 - core).wait_recv()

            when_owner(z_peer(d), relayed)
        for h in range(2):
            grad_two_out[h * share : (h + 1) * share, q * width : (q + 1) * width] = full[q, h]


def on_device(ns, nz, waveform, lengths, conv_one, conv_two, gain_one, shift_one, gain_two, shift_two, cotangent):
    clips, samples = waveform.shape
    channels = conv_two.shape[1]
    half = cotangent.shape[1]
    rows = clips * half
    share = conv_two.shape[0] // ns // 2
    pieces = min(nz, share // 16)
    piece = share // pieces
    width = channels // PARTS
    dma = pltpu.SemaphoreType.DMA
    vmem = pl.BlockSpec(memory_space=pltpu.VMEM)
    hbm = pl.BlockSpec(memory_space=pltpu.HBM)
    features, grad_one, grad_two, norms = pl.pallas_call(
        functools.partial(kernel, ns, nz, pieces),
        out_shape=(
            jax.ShapeDtypeStruct((rows, channels), BF16),
            jax.ShapeDtypeStruct((TAPS, channels), F32),
            jax.ShapeDtypeStruct((2 * share, channels), BF16),
            jax.ShapeDtypeStruct((4, channels), F32),
        ),
        in_specs=[hbm] * 9,
        out_specs=(vmem,) * 4,
        scratch_shapes=[
            pltpu.VMEM(waveform.shape, BF16),
            pltpu.SMEM(lengths.shape, jnp.int32),
            pltpu.VMEM(conv_one.shape, BF16),
            pltpu.VMEM(conv_two.shape, BF16),
            pltpu.VMEM((1, channels), F32),
            pltpu.VMEM((1, channels), F32),
            pltpu.VMEM((1, channels), F32),
            pltpu.VMEM((1, channels), F32),
            pltpu.VMEM((rows, channels), BF16),
            dma((9,)),
            pltpu.VMEM((clips, 128), BF16),
            pltpu.VMEM((2 * rows, 128), F32),
            pltpu.VMEM((2 * rows, channels), F32),
            pltpu.VMEM((2 * rows, channels), F32),
            pltpu.VMEM((2 * rows, 128), F32),
            pltpu.VMEM((2 * rows, channels), F32),
            pltpu.VMEM((clips, half + 8, channels), F32),
            pltpu.VMEM((rows, 3 * channels), BF16),
            pltpu.VMEM((rows, channels), F32),
            pltpu.VMEM((rows, channels), BF16),
            pltpu.VMEM((clips, half + 8, channels), F32),
            pltpu.VMEM((2 * rows, channels), F32),
            pltpu.VMEM((2 * rows, channels), BF16),
            pltpu.VMEM((2 * rows, channels), BF16),
            pltpu.VMEM((PARTS, 2, ns, share, width), BF16),
            pltpu.VMEM((PARTS, ns, share, width), BF16),
            pltpu.VMEM((PARTS, ns - 1, share, width), BF16),
            pltpu.VMEM((PARTS, ns - 1, share, width), BF16),
            pltpu.VMEM((PARTS, share, width), BF16),
            pltpu.VMEM((PARTS, nz - 1, piece, width), BF16),
            pltpu.VMEM((PARTS, 2, share, width), BF16),
            pltpu.VMEM((2, 16, channels // 2), F32),
            pltpu.VMEM((16, channels // 2), F32),
            pltpu.VMEM((16, channels // 2), BF16),
            pltpu.VMEM((ns, 16, channels // 2), BF16),
            pltpu.VMEM((16, channels // 2), BF16),
            pltpu.VMEM((nz, 16, channels // 2), BF16),
            pltpu.VMEM((2, 16, channels // 2), F32),
            dma, dma,
            dma((PARTS, ns)), dma((PARTS, ns)),
            dma((PARTS, ns - 1)), dma((PARTS, ns - 1)),
            dma((PARTS, nz - 1)), dma((PARTS, nz - 1)),
            dma((PARTS, nz - 1)), dma((PARTS, nz - 1)),
            dma((PARTS, nz)), dma((PARTS, nz)),
            dma, dma,
            dma((ns - 1,)), dma((ns - 1,)),
            dma((nz - 1,)), dma((nz - 1,)),
            dma, dma,
        ],
        compiler_params=pltpu.CompilerParams(
            collective_id=0, has_side_effects=True, vmem_limit_bytes=48 * 1024 * 1024
        ),
    )(
        *[
            pltpu.with_memory_space_constraint(value, pltpu.HBM)
            for value in (
        waveform,
        lengths,
        conv_one,
        conv_two,
        gain_one.reshape(1, channels),
        shift_one.reshape(1, channels),
        gain_two.reshape(1, channels),
        shift_two.reshape(1, channels),
        cotangent.reshape(rows, channels),
    )])
    features, grad_one, grad_two, norms = pl.pallas_call(
        put_out,
        out_shape=(
            jax.ShapeDtypeStruct((rows, channels), BF16),
            jax.ShapeDtypeStruct((TAPS, channels), F32),
            jax.ShapeDtypeStruct((2 * share, channels), F32),
            jax.ShapeDtypeStruct((4, channels), F32),
        ),
        in_specs=[vmem] * 4,
        out_specs=(hbm,) * 4,
        scratch_shapes=[pltpu.VMEM((2 * share, channels), F32), dma((4,))],
        compiler_params=pltpu.CompilerParams(vmem_limit_bytes=4 * 1024 * 1024),
    )(features, grad_one, grad_two, norms)
    return features.reshape(clips, half, channels), grad_one, grad_two, norms


def put_out(features, grad_one, grad_two, norms, features_out, grad_one_out, grad_two_out, norms_out, wide, sem):
    copies = [
        pltpu.make_async_copy(source, target, sem.at[i])
        for i, (source, target) in enumerate(
            (
                (features, features_out),
                (grad_one, grad_one_out),
                (norms, norms_out),
                (wide, grad_two_out),
            )
        )
    ]
    for copy in copies[:3]:
        copy.start()
    wide[...] = grad_two[...].astype(F32)
    copies[3].start()
    for copy in copies:
        copy.wait()


def solution(mesh):
    in_specs = (P("dp", "seq"), P("dp", None), P(), P(), P(), P(), P(), P(), P("dp", "seq", None))
    out_specs = (P("dp", "seq", None), P(), P("seq", None), P())
    return jax.shard_map(
        functools.partial(on_device, mesh.shape["seq"], mesh.shape["dp"] // 2),
        mesh=mesh, in_specs=in_specs, out_specs=out_specs, check_vma=False,
    )
```
